32 devices in a mesh: gx: 2 (over y), gy: 4 (over x, core), gz: 4 (over z).
Axes of the slice: x: 2, y: 2, z: 4, core: 2. Of those that a mesh axis runs over, the one named last changes fastest.
Arguments:
- velocity: float32 [3, 20, 80, 2560], P(None, 'gx', 'gy', 'gz'), may hold values from -6 to 6
- obstacle_element_mask: int32 [4, 16, 512], P('gx', 'gy', 'gz'), may hold values 0 or 1
- element_metric_scale: float32 [4, 16, 512], P('gx', 'gy', 'gz'), may hold values from 0.5 to 8
Outputs:
- smoothed: float32 [20, 80, 2560], P('gx', 'gy', 'gz')
- coarse: float32 [4, 16, 512], P('gx', 'gy', 'gz')
The draws below stay inside these ranges and needn't reach their ends.
All inputs are finite; a program needn't handle non-finite values. No bound on the sum of `obstacle_element_mask` on one device may be relied on, other than what follows from the above.
Results may differ from the reference program's by a relative error of at most 0.00012.
Values sent between devices are 32-bit elements; how exact they have to be, the bound alone decides.
A program may use at most 384 MiB of HBM per device.

```python
import math
import jax
import jax.numpy as jnp
import numpy as np
from jax import lax

ELEMENTS_X = 4
ELEMENTS_Y = 16
ELEMENTS_Z = 512
NX = 20
NY = 80
NZ = 2560


def plant(values, stream_key, least, top_value):
    shape = values.shape
    spot = [jax.random.randint(jax.random.fold_in(stream_key, axis), (), 0, shape[axis]) for axis in range(len(shape))]
    values = values.at[tuple(spot)].set(least)
    longest = shape.index(max(shape))
    spot[longest] = (spot[longest] + 1) % shape[longest]
    return values.at[tuple(spot)].set(top_value)


def block_levels(own_key, dims, cuts, smallest, largest):
    def one(dim, blocks):
        draws = jax.random.uniform(jax.random.fold_in(jax.random.fold_in(own_key, 6), dim), (blocks,), jnp.float32, smallest / len(cuts), largest / len(cuts))
        return jnp.repeat(jnp.exp(draws), dims[dim] // blocks).reshape((-1,) + (1,) * (len(dims) - dim - 1))

    factor_of = one(*cuts[0])
    for cut in cuts[1:]:
        factor_of = factor_of * one(*cut)
    return factor_of


def bell_draw(key, shape, spread, most, cuts=(), kind=jnp.bfloat16):
    entries = jax.random.normal(key, shape, jnp.float32) * spread
    if len(cuts) > 0:
        entries = block_levels(key, shape, cuts, -0.22, 0.18) * entries
    return jnp.clip(entries, min=-most, max=most).astype(kind)


def setup_inputs(seed: int = 0) -> dict:
    seeds = jax.random.split(jax.random.key(seed), 4)
    velocity = bell_draw(seeds[0], (3, NX, NY, NZ), 1.0, 6.0, ((1, 2), (2, 4), (3, 4)), jnp.float32)
    obstacle_element_mask = plant((jax.random.randint(seeds[1], (ELEMENTS_X, ELEMENTS_Y, ELEMENTS_Z), 0, 8) < 1).astype(jnp.int32), jax.random.fold_in(seeds[1], 1), 0, 1)
    element_metric_scale = jnp.clip(jnp.exp(math.log(8.0) - 2.7725887 * jax.random.uniform(seeds[2], (ELEMENTS_X, ELEMENTS_Y, ELEMENTS_Z), jnp.float32) ** block_levels(seeds[2], (ELEMENTS_X, ELEMENTS_Y, ELEMENTS_Z), ((0, 2), (1, 4), (2, 4)), -0.2, 0.2)), 0.5, 8.0)
    return dict(velocity=velocity, obstacle_element_mask=obstacle_element_mask, element_metric_scale=element_metric_scale)


lift_factor = 10.0
time_step = 0.05
penalty = 4.0

def lobatto_points():
    return np.array([-1.0, -math.sqrt(3.0 / 7.0), 0.0, math.sqrt(3.0 / 7.0), 1.0])

def lobatto_weights():
    return np.array([0.1, 49.0 / 90.0, 32.0 / 45.0, 49.0 / 90.0, 0.1])

def derivative_matrix():
    points = lobatto_points()
    scales = np.array([np.prod([points[i] - points[k] for k in range(5) if k != i]) for i in range(5)])
    result = np.zeros((5, 5))
    for i in range(5):
        for j in range(5):
            if i != j:
                result[i, j] = scales[i] / (scales[j] * (points[i] - points[j]))
        result[i, i] = -np.sum(result[i])
    return result

def eigen_basis_table():
    return np.array([[math.sqrt((1.0 if k == 0 else 2.0) / 5.0) * math.cos(math.pi * (i + 0.5) * k / 5.0) for k in range(5)] for i in range(5)])

def eigen_value_table():
    return np.array([4.0 * math.sin(math.pi * k / 10.0) ** 2 for k in range(5)])

def hat_weight_table():
    points = lobatto_points()
    weights = lobatto_weights()
    return np.array([weights * (1.0 - points) / 2.0, weights * (1.0 + points) / 2.0])

def apply_along(matrix, field, axis):
    weights = jnp.asarray(matrix, jnp.float32)
    out_width = weights.shape[0]
    in_width = weights.shape[1]
    extent = field.shape
    if axis == 0:
        blocks = field.reshape(extent[0] // in_width, in_width, extent[1], extent[2])
        result = jnp.einsum('ij,ajbc->aibc', weights, blocks, precision=lax.Precision.HIGHEST)
        return result.reshape(extent[0] // in_width * out_width, extent[1], extent[2])
    if axis == 1:
        blocks = field.reshape(extent[0], extent[1] // in_width, in_width, extent[2])
        result = jnp.einsum('ij,abjc->abic', weights, blocks, precision=lax.Precision.HIGHEST)
        return result.reshape(extent[0], extent[1] // in_width * out_width, extent[2])
    blocks = field.reshape(extent[0], extent[1], extent[2] // in_width, in_width)
    result = jnp.einsum('ij,abcj->abci', weights, blocks, precision=lax.Precision.HIGHEST)
    return result.reshape(extent[0], extent[1], extent[2] // in_width * out_width)

def to_nodes(values):
    return jnp.repeat(jnp.repeat(jnp.repeat(values, 5, axis=0), 5, axis=1), 5, axis=2)

def face_masks(extent, axis):
    position = jnp.arange(extent) % 5
    layout = [1, 1, 1]
    layout[axis] = extent
    left_end = (position == 0).astype(jnp.float32).reshape(layout)
    right_end = (position == 4).astype(jnp.float32).reshape(layout)
    return (left_end, right_end)

def neighbours(padded, axis):
    inner = padded[1:-1, 1:-1, 1:-1]
    extent = inner.shape[axis]
    lower = [slice(1, -1)] * 3
    upper = [slice(1, -1)] * 3
    lower[axis] = slice(0, extent)
    upper[axis] = slice(2, extent + 2)
    return (inner, padded[tuple(lower)], padded[tuple(upper)])

def convective(padded):
    dmatrix = derivative_matrix()
    terms = []
    for c in range(3):
        total = jnp.zeros(padded.shape[1:], jnp.float32)[1:-1, 1:-1, 1:-1]
        for a in range(3):
            normal_in, normal_lo, normal_hi = neighbours(padded[a], a)
            moved_in, moved_lo, moved_hi = neighbours(padded[c], a)
            flux_in = normal_in * moved_in
            left_end, right_end = face_masks(normal_in.shape[a], a)
            speed_lo = jnp.maximum(jnp.abs(normal_in), jnp.abs(normal_lo))
            speed_hi = jnp.maximum(jnp.abs(normal_in), jnp.abs(normal_hi))
            jump_lo = -0.5 * (normal_lo * moved_lo - flux_in) - 0.5 * speed_lo * (moved_lo - moved_in)
            upper_jump_value = 0.5 * (normal_hi * moved_hi - flux_in) - 0.5 * speed_hi * (moved_hi - moved_in)
            total = total + apply_along(dmatrix, flux_in, a) + lift_factor * (left_end * jump_lo + right_end * upper_jump_value)
        terms.append(total)
    return terms

def divergence(triples):
    dmatrix = derivative_matrix()
    total = 0.0
    for a in range(3):
        inner, lower, upper = triples[a]
        left_end, right_end = face_masks(inner.shape[a], a)
        total = total + apply_along(dmatrix, inner, a) + lift_factor * (left_end * -0.5 * (lower - inner) + right_end * 0.5 * (upper - inner))
    return total

def smooth(pressure_right_side, element_metric_scale):
    basis = eigen_basis_table()
    coeffs = pressure_right_side
    for axis in range(3):
        coeffs = apply_along(basis.T, coeffs, axis)
    extent = pressure_right_side.shape
    modal = jnp.asarray(eigen_value_table(), jnp.float32)
    modes = jnp.tile(modal, extent[0] // 5)[:, None, None] + jnp.tile(modal, extent[1] // 5)[None, :, None] + jnp.tile(modal, extent[2] // 5)[None, None, :]
    coeffs = coeffs / (to_nodes(element_metric_scale) * modes + 1.0)
    for axis in range(3):
        coeffs = apply_along(basis, coeffs, axis)
    return coeffs

def vertex_partials(pressure_right_side):
    hats = hat_weight_table()
    reduced = pressure_right_side
    for axis in range(3):
        reduced = apply_along(hats, reduced, axis)
    extent = reduced.shape
    blocks = reduced.reshape(extent[0] // 2, 2, extent[1] // 2, 2, extent[2] // 2, 2)
    corner_vertex_list = 0.0
    for a in range(2):
        for b in range(2):
            for c in range(2):
                corner_vertex_list = corner_vertex_list + jnp.pad(blocks[:, a, :, b, :, c], ((a, 1 - a), (b, 1 - b), (c, 1 - c)))
    return corner_vertex_list

def reference(velocity, obstacle_element_mask, element_metric_scale):
    padded = jnp.pad(velocity, ((0, 0), (1, 1), (1, 1), (1, 1)))
    damping = 1.0 + penalty * to_nodes(obstacle_element_mask.astype(jnp.float32))
    terms = convective(padded)
    provisional = jnp.stack([(velocity[c] - time_step * terms[c]) / damping for c in range(3)])
    widened = jnp.pad(provisional, ((0, 0), (1, 1), (1, 1), (1, 1)))
    triples = [neighbours(widened[a], a) for a in range(3)]
    pressure_right_side = -divergence(triples)
    smoothed = smooth(pressure_right_side, element_metric_scale)
    corner_vertex_list = vertex_partials(pressure_right_side)
    coarse = corner_vertex_list[:-1, :-1, :-1]
    return (smoothed, coarse)
```

```python
import functools
import itertools
import math

import jax
import jax.numpy as jnp
import numpy as np
from jax import lax
from jax.experimental import pallas as pl
from jax.experimental.pallas import tpu as pltpu
from jax.sharding import PartitionSpec as P

lift_factor = 10.0
time_step = 0.05
penalty = 4.0
half_lift = lift_factor * 0.5
order = 5
names = ("gx", "gy", "gz")
corners = [s for s in itertools.product((0, 1), repeat=3) if any(s)]


def lobatto_points():
    return np.array([-1.0, -math.sqrt(3.0 / 7.0), 0.0, math.sqrt(3.0 / 7.0), 1.0])


def lobatto_weights():
    return np.array([0.1, 49.0 / 90.0, 32.0 / 45.0, 49.0 / 90.0, 0.1])


def derivative_matrix():
    points = lobatto_points()
    scales = np.array(
        [np.prod([points[i] - points[k] for k in range(5) if k != i]) for i in range(5)]
    )
    result = np.zeros((5, 5))
    for i in range(5):
        for j in range(5):
            if i != j:
                result[i, j] = scales[i] / (scales[j] * (points[i] - points[j]))
        result[i, i] = -np.sum(result[i])
    return result


def eigen_basis_table():
    return np.array(
        [
            [
                math.sqrt((1.0 if k == 0 else 2.0) / 5.0) * math.cos(math.pi * (i + 0.5) * k / 5.0)
                for k in range(5)
            ]
            for i in range(5)
        ]
    )


def eigen_value_table():
    return np.array([4.0 * math.sin(math.pi * k / 10.0) ** 2 for k in range(5)])


def hat_weight_table():
    points = lobatto_points()
    weights = lobatto_weights()
    return np.array([weights * (1.0 - points) / 2.0, weights * (1.0 + points) / 2.0])


def mix(coefs, terms):
    total = None
    for coef, term in zip(coefs, terms):
        if abs(coef) < 1e-12:
            continue
        piece = float(coef) * term
        total = piece if total is None else total + piece
    return total


def lifted_derivative(f):
    d = derivative_matrix()
    d[0, 0] += half_lift
    d[4, 4] -= half_lift
    e1, e2 = f[0] + f[4], f[1] + f[3]
    o1, o2 = f[0] - f[4], f[1] - f[3]
    out = [None] * 5
    for i in range(2):
        even = mix(((d[i, 0] + d[i, 4]) / 2, (d[i, 1] + d[i, 3]) / 2, d[i, 2]), (e1, e2, f[2]))
        odd = mix(((d[i, 0] - d[i, 4]) / 2, (d[i, 1] - d[i, 3]) / 2), (o1, o2))
        out[i] = odd + even
        out[4 - i] = odd - even
    out[2] = mix((d[2, 0], d[2, 1]), (o1, o2))
    return out


def to_modes(f):
    s = eigen_basis_table()
    e1, e2 = f[0] + f[4], f[1] + f[3]
    o1, o2 = f[0] - f[4], f[1] - f[3]
    out = []
    for k in range(5):
        if k == 0:
            out.append(float(s[0, 0]) * (e1 + e2 + f[2]))
        elif k % 2 == 0:
            out.append(mix((s[0, k], s[1, k], s[2, k]), (e1, e2, f[2])))
        else:
            out.append(mix((s[0, k], s[1, k]), (o1, o2)))
    return out


def from_modes(c):
    s = eigen_basis_table()
    out = [None] * 5
    base = float(s[0, 0]) * c[0]
    for i in range(2):
        even = base + mix((s[i, 2], s[i, 4]), (c[2], c[4]))
        odd = mix((s[i, 1], s[i, 3]), (c[1], c[3]))
        out[i] = even + odd
        out[4 - i] = even - odd
    out[2] = base + mix((s[2, 2], s[2, 4]), (c[2], c[4]))
    return out


def at_line(a, l, m):
    return ((l, m), (m, l), (m, slice(None), l))[a]


def roll(x, shift, axis):
    size = x.shape[axis]
    shift = shift % size
    return x if shift == 0 else pltpu.roll(x, shift, axis)


class Brick:
    def __init__(self, ex, ey, ez):
        self.ex, self.ey, self.ez = ex, ey, ez
        self.rows = ex * ey

    def iotas(self):
        row = lax.broadcasted_iota(jnp.int32, (self.rows, self.ez), 0)
        lane = lax.broadcasted_iota(jnp.int32, (self.rows, self.ez), 1)
        return row, lane

    def slots(self, a):
        return (self.ex, self.ey, self.ez)[a]

    def packed(self, a, n):
        return -(-n // self.slots(a))

    def step(self, a):
        return (self.ey, 1, 1)[a]

    def place(self, a):
        row, lane = self.iotas()
        return (row // self.ey, row % self.ey, lane)[a]

    def pack(self, face, a, up):
        n = face.shape[0]
        slots, step = self.slots(a), self.step(a)
        axis = 2 if a == 2 else 1
        place = self.place(a)
        start = slots - 1 if up else 0
        groups = []
        if a == 2:
            total = jnp.zeros((self.rows, self.ez), jnp.float32)
            for s in range(n):
                total = jnp.where(place == s, roll(face[s], s - start, 1), total)
            return total[None]
        for g in range(self.packed(a, n)):
            total = None
            for s in range(min(slots, n - g * slots)):
                piece = roll(face[g * slots + s], (s - start) * step, 0)
                total = piece if total is None else jnp.where(place == s, piece, total)
            groups.append(total)
        return jnp.stack(groups)

    def entry(self, packed_ref, n, a, up):
        slots, step = self.slots(a), self.step(a)
        target = 0 if up else slots - 1
        g, s = divmod(n, slots)
        return roll(packed_ref[g], (target - s) * step, 1 if a == 2 else 0)

    def move(self, x, a, up):
        step = self.step(a) if up else -self.step(a)
        return roll(x, step, 1 if a == 2 else 0)

    def edge(self, a, up):
        return self.place(a) == (0 if up else self.slots(a) - 1)


def body(
    brick,
    counts,
    v_ref,
    mask_ref,
    scale_ref,
    smooth_ref,
    coarse_ref,
    rows_buf,
    vel,
    conv,
    near,
    pres,
    *rest,
):
    send1, recv1, send2, recv2 = rest[0:6], rest[6:12], rest[12:18], rest[18:24]
    send3, recv3 = rest[24], rest[25]
    ssem1, rsem1, ssem2, rsem2, ssem3, rsem3 = rest[26:32]
    ex, ey, ez = brick.ex, brick.ey, brick.ez
    ny = ey * order
    me = [lax.axis_index(name) for name in names]

    def offset_id(shift):
        return tuple(me[a] + shift[a] for a in range(3))

    def exists(shift):
        ok = None
        for a in range(3):
            if shift[a] > 0:
                one = me[a] < counts[a] - 1
            elif shift[a] < 0:
                one = me[a] > 0
            else:
                continue
            ok = one if ok is None else jnp.logical_and(ok, one)
        return ok

    unit = [tuple(int(a == b) for b in range(3)) for a in range(3)]
    partners = [s for s in corners] + [tuple(-x for x in s) for s in corners]
    barrier = pltpu.get_barrier_semaphore()
    for shift in partners:

        @pl.when(exists(shift))
        def _():
            pl.semaphore_signal(
                barrier,
                inc=1,
                device_id=offset_id(shift),
                device_id_type=pl.DeviceIdType.MESH,
            )

    def copies(send, recv, ssem, rsem):
        out = []
        for a in range(3):
            for s in range(2):
                d = 2 * a + s
                sign = 1 - 2 * s
                to = tuple(sign * u for u in unit[a])
                source = tuple(-sign * u for u in unit[a])
                copy = pltpu.make_async_remote_copy(
                    src_ref=send[d],
                    dst_ref=recv[d],
                    send_sem=ssem.at[d],
                    recv_sem=rsem.at[d],
                    device_id=offset_id(to),
                    device_id_type=pl.DeviceIdType.MESH,
                )
                out.append((copy, exists(to), exists(source), recv[d]))
        return out

    def start(group):
        for copy, has_to, has_source, _ in group:

            @pl.when(has_to)
            def _():
                copy.start()

    def clear(group):
        for _, _, has_source, dst in group:

            @pl.when(jnp.logical_not(has_source))
            def _():
                dst[...] = jnp.zeros_like(dst)

    def arrive(group):
        for copy, has_to, has_source, _ in group:

            @pl.when(has_source)
            def _():
                copy.wait_recv()

    def finish(group):
        for copy, has_to, has_source, _ in group:

            @pl.when(has_to)
            def _():
                copy.wait_send()

    round1 = copies(send1, recv1, ssem1, rsem1)
    round2 = copies(send2, recv2, ssem2, rsem2)
    round3 = []
    for n, shift in enumerate(corners):
        copy = pltpu.make_async_remote_copy(
            src_ref=send3.at[n],
            dst_ref=recv3.at[n],
            send_sem=ssem3.at[n],
            recv_sem=rsem3.at[n],
            device_id=offset_id(shift),
            device_id_type=pl.DeviceIdType.MESH,
        )
        back = tuple(-x for x in shift)
        round3.append((copy, exists(shift), exists(back), recv3.at[n]))

    row, lane = brick.iotas()
    spread = pow(order, -1, ez)
    gather_index = (lane * order) % ez
    scatter_index = (lane * spread) % ez

    def permute(x, index):
        return jnp.take_along_axis(x, index, axis=1, mode="promise_in_bounds")

    tile_of = [(((lane - spread * k) % ez) * order + k) // ez for k in range(order)]

    def split(i, carry):
        for c in range(3):
            for t in range(order):
                for x in range(ex):
                    rows_buf[c, i, t, x * ny : (x + 1) * ny, :] = v_ref[
                        c, x * order + i, :, t * ez : (t + 1) * ez
                    ]
            for j in range(order):
                parts = [
                    permute(rows_buf[c, i, t, pl.ds(j, brick.rows, stride=order), :], gather_index)
                    for t in range(order)
                ]
                for k in range(order):
                    total = parts[0]
                    for t in range(1, order):
                        total = jnp.where(tile_of[k] == t, parts[t], total)
                    vel[c, i, j, k] = roll(total, -spread * k, 1)
        return carry

    lax.fori_loop(0, order, split, 0)

    clear(round1)
    clear(round2)
    clear(round3)
    faces = order * order

    def face_of(ref, a, l):
        index = ((l,), (slice(None), l), (slice(None), slice(None), l))[a]
        return ref[index]

    for a in range(3):
        for s in range(2):
            l = order - 1 if s == 0 else 0
            face = jnp.concatenate(
                [
                    face_of(vel.at[c], a, l).reshape(faces, brick.rows, ez)
                    for c in range(3)
                ]
            )
            send1[2 * a + s][...] = brick.pack(face, a, s == 0)

    pl.semaphore_wait(barrier, sum(exists(shift).astype(jnp.int32) for shift in partners))

    start(round1)

    def inner_axis(a):
        def run(m, carry):
            normal = [vel[(a,) + at_line(a, l, m)] for l in range(order)]
            for c in range(3):
                if c == a:
                    flux = [x * x for x in normal]
                else:
                    flux = [normal[l] * vel[(c,) + at_line(a, l, m)] for l in range(order)]
                out = lifted_derivative(flux)
                for l in range(order):
                    where = (c,) + at_line(a, l, m)
                    conv[where] = out[l] if a == 0 else conv[where] + out[l]
            return carry

        lax.fori_loop(0, order, run, 0)

    for a in range(3):
        inner_axis(a)

    arrive(round1)

    for a in range(3):
        for s in range(2):
            up = s == 0
            edge = brick.edge(a, up)
            own, other = (0, order - 1) if up else (order - 1, 0)
            for c in range(3):
                for m in range(order):
                    line = vel[(c,) + at_line(a, other, m)]
                    for q in range(order):
                        n = (c * order + m) * order + q
                        far = brick.entry(recv1[2 * a + s], n, a, up)
                        near[c, m, q] = jnp.where(edge, far, brick.move(line[q], a, up))

            def add_faces(m, carry):
                normal = vel[(a,) + at_line(a, own, m)]
                normal_out = near[a, m]
                speed = jnp.maximum(jnp.abs(normal), jnp.abs(normal_out))
                for c in range(3):
                    moved = vel[(c,) + at_line(a, own, m)]
                    moved_out = near[c, m]
                    jump = speed * (moved_out - moved)
                    flux = normal_out * moved_out
                    where = (c,) + at_line(a, own, m)
                    if up:
                        conv[where] = conv[where] - half_lift * (flux + jump)
                    else:
                        conv[where] = conv[where] + half_lift * (flux - jump)
                return carry

            lax.fori_loop(0, order, add_faces, 0)

    solid = jnp.concatenate([mask_ref[x] for x in range(ex)], axis=0).astype(jnp.float32)
    scale = jnp.concatenate([scale_ref[x] for x in range(ex)], axis=0)
    fluid = 1.0 / (1.0 + penalty * solid)

    def advance(i, carry):
        for c in range(3):
            conv[c, i] = (vel[c, i] - time_step * conv[c, i]) * fluid
        return carry

    lax.fori_loop(0, order, advance, 0)

    for a in range(3):
        for s in range(2):
            l = order - 1 if s == 0 else 0
            face = face_of(conv.at[a], a, l).reshape(faces, brick.rows, ez)
            send2[2 * a + s][...] = brick.pack(face, a, s == 0)
    start(round2)

    for a in range(3):

        def diverge(m, carry):
            out = lifted_derivative([conv[(a,) + at_line(a, l, m)] for l in range(order)])
            for l in range(order):
                where = at_line(a, l, m)
                pres[where] = -out[l] if a == 0 else pres[where] - out[l]
            return carry

        lax.fori_loop(0, order, diverge, 0)

    arrive(round2)
    for a in range(3):
        for s in range(2):
            up = s == 0
            edge = brick.edge(a, up)
            own, other = (0, order - 1) if up else (order - 1, 0)
            for m in range(order):
                line = conv[(a,) + at_line(a, other, m)]
                values = []
                for q in range(order):
                    far = brick.entry(recv2[2 * a + s], m * order + q, a, up)
                    values.append(jnp.where(edge, far, brick.move(line[q], a, up)))
                side = jnp.stack(values)
                where = at_line(a, own, m)
                if up:
                    pres[where] = pres[where] + half_lift * side
                else:
                    pres[where] = pres[where] - half_lift * side

    hats = hat_weight_table()
    by_x = []
    for i in range(order):
        slab = [pres[i, j] for j in range(order)]
        along_y = [mix(hats[b], slab) for b in range(2)]
        by_x.append([[mix(hats[c], [along_y[b][k] for k in range(order)]) for c in range(2)] for b in range(2)])
    parts = {
        (a, b, c): mix(hats[a], [by_x[i][b][c] for i in range(order)])
        for a in range(2)
        for b in range(2)
        for c in range(2)
    }
    for a in (2, 1, 0):
        edge = brick.edge(a, True)
        merged = {}
        for key in parts:
            if key[a] == 1:
                continue
            upper = key[:a] + (1,) + key[a + 1 :]
            moved = brick.move(parts[upper], a, True)
            if a == 1:
                swap = roll(parts[upper], 1 - ey, 0)
                moved = jnp.where(edge, swap, moved)
            merged[key] = parts[key] + jnp.where(edge, 0.0, moved)
            merged[upper] = jnp.where(edge, moved, 0.0)
        parts = merged
    for n, shift in enumerate(corners):
        send3[n] = parts[shift]
    start(round3)

    basis_values = eigen_value_table()

    def forward(i, carry):
        slab = to_modes([pres[i, j] for j in range(order)])
        for j in range(order):
            out = to_modes([slab[j][k] for k in range(order)])
            for k in range(order):
                pres[i, j, k] = out[k]
        return carry

    lax.fori_loop(0, order, forward, 0)

    for j in range(order):
        modes = to_modes([pres[i, j] for i in range(order)])
        scaled = []
        for i in range(order):
            denominator = jnp.stack(
                [
                    scale * float(basis_values[i] + basis_values[j] + basis_values[k]) + 1.0
                    for k in range(order)
                ]
            )
            scaled.append(modes[i] / denominator)
        out = from_modes(scaled)
        for i in range(order):
            pres[i, j] = out[i]

    def backward(i, carry):
        slab = from_modes([pres[i, j] for j in range(order)])
        for j in range(order):
            out = from_modes([slab[j][k] for k in range(order)])
            rolled = [roll(out[k], spread * k, 1) for k in range(order)]
            for t in range(order):
                total = rolled[0]
                for k in range(1, order):
                    total = jnp.where(tile_of[k] == t, rolled[k], total)
                rows_buf[0, i, t, pl.ds(j, brick.rows, stride=order), :] = permute(
                    total, scatter_index
                )
        for t in range(order):
            for x in range(ex):
                smooth_ref[x * order + i, :, t * ez : (t + 1) * ez] = rows_buf[
                    0, i, t, x * ny : (x + 1) * ny, :
                ]
        return carry

    lax.fori_loop(0, order, backward, 0)

    arrive(round3)
    total = parts[(0, 0, 0)]
    for n in range(len(corners)):
        total = total + recv3[n]
    for x in range(ex):
        coarse_ref[x] = total[x * ey : (x + 1) * ey]
    finish(round1)
    finish(round2)
    finish(round3)


def shards(counts, velocity, mask, scale):
    ex, ey, ez = mask.shape
    brick = Brick(ex, ey, ez)
    tile = (brick.rows, ez)
    faces = order * order

    def buffers(n):
        return [
            pltpu.VMEM((brick.packed(a, n),) + tile, jnp.float32)
            for a in range(3)
            for _ in range(2)
        ]

    whole = pl.BlockSpec(memory_space=pltpu.VMEM)
    sems = pltpu.SemaphoreType.DMA
    return pl.pallas_call(
        functools.partial(body, brick, counts),
        out_shape=(
            jax.ShapeDtypeStruct(velocity.shape[1:], jnp.float32),
            jax.ShapeDtypeStruct(mask.shape, jnp.float32),
        ),
        in_specs=[whole] * 3,
        out_specs=(whole, whole),
        scratch_shapes=[
            pltpu.VMEM((3, order, order, brick.rows * order, ez), jnp.float32),
            pltpu.VMEM((3, order, order, order) + tile, jnp.float32),
            pltpu.VMEM((3, order, order, order) + tile, jnp.float32),
            pltpu.VMEM((3, order, order) + tile, jnp.float32),
            pltpu.VMEM((order, order, order) + tile, jnp.float32),
        ]
        + buffers(3 * faces)
        + buffers(3 * faces)
        + buffers(faces)
        + buffers(faces)
        + [
            pltpu.VMEM((len(corners),) + tile, jnp.float32),
            pltpu.VMEM((len(corners),) + tile, jnp.float32),
        ]
        + [sems((6,)), sems((6,)), sems((6,)), sems((6,)), sems((7,)), sems((7,))],
        compiler_params=pltpu.CompilerParams(
            collective_id=0, has_side_effects=True, vmem_limit_bytes=40 * 2**20
        ),
    )(velocity, mask, scale)


def solution(mesh):
    counts = tuple(mesh.shape[name] for name in names)
    return jax.shard_map(
        functools.partial(shards, counts),
        mesh=mesh,
        in_specs=(P(None, "gx", "gy", "gz"), P("gx", "gy", "gz"), P("gx", "gy", "gz")),
        out_specs=(P("gx", "gy", "gz"), P("gx", "gy", "gz")),
        check_vma=False,
    )
```

```python
import functools
import itertools
import math

import jax
import jax.numpy as jnp
import numpy as np
from jax import lax
from jax.experimental import pallas as pl
from jax.experimental.pallas import tpu as pltpu
from jax.sharding import PartitionSpec as P

lift_factor = 10.0
time_step = 0.05
penalty = 4.0
half_lift = lift_factor * 0.5
order = 5
names = ("gx", "gy", "gz")
corners = [s for s in itertools.product((0, 1), repeat=3) if any(s)]


def lobatto_points():
    return np.array([-1.0, -math.sqrt(3.0 / 7.0), 0.0, math.sqrt(3.0 / 7.0), 1.0])


def lobatto_weights():
    return np.array([0.1, 49.0 / 90.0, 32.0 / 45.0, 49.0 / 90.0, 0.1])


def derivative_matrix():
    points = lobatto_points()
    scales = np.array(
        [np.prod([points[i] - points[k] for k in range(5) if k != i]) for i in range(5)]
    )
    result = np.zeros((5, 5))
    for i in range(5):
        for j in range(5):
            if i != j:
                result[i, j] = scales[i] / (scales[j] * (points[i] - points[j]))
        result[i, i] = -np.sum(result[i])
    return result


def eigen_basis_table():
    return np.array(
        [
            [
                math.sqrt((1.0 if k == 0 else 2.0) / 5.0) * math.cos(math.pi * (i + 0.5) * k / 5.0)
                for k in range(5)
            ]
            for i in range(5)
        ]
    )


def eigen_value_table():
    return np.array([4.0 * math.sin(math.pi * k / 10.0) ** 2 for k in range(5)])


def hat_weight_table():
    points = lobatto_points()
    weights = lobatto_weights()
    return np.array([weights * (1.0 - points) / 2.0, weights * (1.0 + points) / 2.0])


def mix(coefs, terms):
    total = None
    for coef, term in zip(coefs, terms):
        if abs(coef) < 1e-12:
            continue
        piece = float(coef) * term
        total = piece if total is None else total + piece
    return total


def lifted_derivative(f):
    d = derivative_matrix()
    d[0, 0] += half_lift
    d[4, 4] -= half_lift
    e1, e2 = f[0] + f[4], f[1] + f[3]
    o1, o2 = f[0] - f[4], f[1] - f[3]
    out = [None] * 5
    for i in range(2):
        even = mix(((d[i, 0] + d[i, 4]) / 2, (d[i, 1] + d[i, 3]) / 2, d[i, 2]), (e1, e2, f[2]))
        odd = mix(((d[i, 0] - d[i, 4]) / 2, (d[i, 1] - d[i, 3]) / 2), (o1, o2))
        out[i] = odd + even
        out[4 - i] = odd - even
    out[2] = mix((d[2, 0], d[2, 1]), (o1, o2))
    return out


def to_modes(f):
    s = eigen_basis_table()
    e1, e2 = f[0] + f[4], f[1] + f[3]
    o1, o2 = f[0] - f[4], f[1] - f[3]
    out = []
    for k in range(5):
        if k == 0:
            out.append(float(s[0, 0]) * (e1 + e2 + f[2]))
        elif k % 2 == 0:
            out.append(mix((s[0, k], s[1, k], s[2, k]), (e1, e2, f[2])))
        else:
            out.append(mix((s[0, k], s[1, k]), (o1, o2)))
    return out


def from_modes(c):
    s = eigen_basis_table()
    out = [None] * 5
    base = float(s[0, 0]) * c[0]
    for i in range(2):
        even = base + mix((s[i, 2], s[i, 4]), (c[2], c[4]))
        odd = mix((s[i, 1], s[i, 3]), (c[1], c[3]))
        out[i] = even + odd
        out[4 - i] = even - odd
    out[2] = base + mix((s[2, 2], s[2, 4]), (c[2], c[4]))
    return out


def at_line(a, l, m):
    return ((l, m), (m, l), (m, slice(None), l))[a]


def roll(x, shift, axis):
    size = x.shape[axis]
    shift = shift % size
    return x if shift == 0 else pltpu.roll(x, shift, axis)


class Brick:
    def __init__(self, ex, ey, ez):
        self.ex, self.ey, self.ez = ex, ey, ez
        self.rows = ex * ey

    def iotas(self):
        row = lax.broadcasted_iota(jnp.int32, (self.rows, self.ez), 0)
        lane = lax.broadcasted_iota(jnp.int32, (self.rows, self.ez), 1)
        return row, lane

    def slots(self, a):
        return (self.ex, self.ey, self.ez)[a]

    def packed(self, a, n):
        return -(-n // self.slots(a))

    def step(self, a):
        return (self.ey, 1, 1)[a]

    def place(self, a):
        row, lane = self.iotas()
        return (row // self.ey, row % self.ey, lane)[a]

    def pack(self, face, a, up):
        n = face.shape[0]
        slots, step = self.slots(a), self.step(a)
        axis = 2 if a == 2 else 1
        place = self.place(a)
        start = slots - 1 if up else 0
        groups = []
        if a == 2:
            total = jnp.zeros((self.rows, self.ez), jnp.float32)
            for s in range(n):
                total = jnp.where(place == s, roll(face[s], s - start, 1), total)
            return total[None]
        for g in range(self.packed(a, n)):
            total = None
            for s in range(min(slots, n - g * slots)):
                piece = roll(face[g * slots + s], (s - start) * step, 0)
                total = piece if total is None else jnp.where(place == s, piece, total)
            groups.append(total)
        return jnp.stack(groups)

    def entry(self, packed_ref, n, a, up):
        slots, step = self.slots(a), self.step(a)
        target = 0 if up else slots - 1
        g, s = divmod(n, slots)
        return roll(packed_ref[g], (target - s) * step, 1 if a == 2 else 0)

    def move(self, x, a, up):
        step = self.step(a) if up else -self.step(a)
        return roll(x, step, 1 if a == 2 else 0)

    def edge(self, a, up):
        return self.place(a) == (0 if up else self.slots(a) - 1)


def body(
    brick,
    counts,
    v_ref,
    mask_ref,
    scale_ref,
    smooth_ref,
    coarse_ref,
    raw,
    mask_buf,
    scale_buf,
    rows_buf,
    vel,
    conv,
    near,
    far_x,
    pres,
    raw_x,
    *rest,
):
    send1, recv1, send2, recv2 = rest[0:4], rest[4:8], rest[8:14], rest[14:20]
    send3, recv3 = rest[20], rest[21]
    ssem1, rsem1, ssem2, rsem2, ssem3, rsem3, load_sem, small_sem, ssemx, rsemx = rest[
        22:32
    ]
    ex, ey, ez = brick.ex, brick.ey, brick.ez
    ny = ey * order
    me = [lax.axis_index(name) for name in names]

    def offset_id(shift):
        return tuple(me[a] + shift[a] for a in range(3))

    def exists(shift):
        ok = None
        for a in range(3):
            if shift[a] > 0:
                one = me[a] < counts[a] - 1
            elif shift[a] < 0:
                one = me[a] > 0
            else:
                continue
            ok = one if ok is None else jnp.logical_and(ok, one)
        return ok

    layers = ex * order
    loads = [
        pltpu.make_async_copy(v_ref.at[:, n], raw.at[:, n], load_sem.at[n]) for n in range(layers)
    ]
    small = [
        pltpu.make_async_copy(mask_ref, mask_buf, small_sem.at[0]),
        pltpu.make_async_copy(scale_ref, scale_buf, small_sem.at[1]),
    ]

    unit = [tuple(int(a == b) for b in range(3)) for a in range(3)]
    partners = unit + [tuple(-x for x in u) for u in unit]
    barrier = pltpu.get_barrier_semaphore()
    for shift in partners:

        @pl.when(exists(shift))
        def _():
            pl.semaphore_signal(
                barrier,
                inc=1,
                device_id=offset_id(shift),
                device_id_type=pl.DeviceIdType.MESH,
            )

    for i in range(order):
        for x in range(ex):
            loads[x * order + i].start()
    for copy in small:
        copy.start()

    def transfer(src, dst, ssem, rsem, to):
        copy = pltpu.make_async_remote_copy(
            src_ref=src,
            dst_ref=dst,
            send_sem=ssem,
            recv_sem=rsem,
            device_id=offset_id(to),
            device_id_type=pl.DeviceIdType.MESH,
        )
        return (copy, exists(to), exists(tuple(-x for x in to)), dst)

    def copies(send, recv, ssem, rsem, axes):
        out = []
        for n, a in enumerate(axes):
            for s in range(2):
                d = 2 * n + s
                to = tuple((1 - 2 * s) * u for u in unit[a])
                out.append(transfer(send[d], recv[d], ssem.at[d], rsem.at[d], to))
        return out

    def start(group):
        for copy, has_to, has_source, _ in group:

            @pl.when(has_to)
            def _():
                copy.start()

    def clear(group):
        for _, _, has_source, dst in group:

            @pl.when(jnp.logical_not(has_source))
            def _():
                dst[...] = jnp.zeros_like(dst)

    def arrive(group):
        for copy, has_to, has_source, _ in group:

            @pl.when(has_source)
            def _():
                copy.wait_recv()

    def finish(group):
        for copy, has_to, has_source, _ in group:

            @pl.when(has_to)
            def _():
                copy.wait_send()

    round1x = []
    for c in range(3):
        for s, n in enumerate((layers - 1, 0)):
            to = tuple((1 - 2 * s) * u for u in unit[0])
            d = 2 * c + s
            round1x.append(
                transfer(v_ref.at[c, n], raw_x.at[s, c], ssemx.at[d], rsemx.at[d], to)
            )
    round1 = copies(send1, recv1, ssem1, rsem1, (1, 2))
    round2 = copies(send2, recv2, ssem2, rsem2, (0, 1, 2))
    round3 = [
        transfer(send3.at[n], recv3.at[n], ssem3.at[n], rsem3.at[n], shift)
        for n, shift in enumerate(corners)
    ]

    row, lane = brick.iotas()
    spread = pow(order, -1, ez)
    gather_index = (lane * order) % ez
    scatter_index = (lane * spread) % ez

    def permute(x, index):
        return jnp.take_along_axis(x, index, axis=1, mode="promise_in_bounds")

    tile_of = [(((lane - spread * k) % ez) * order + k) // ez for k in range(order)]

    def split_layer(slab, rows, put, components=(0, 1, 2)):
        for c in components:
            for t in range(order):
                for x in slab:
                    rows[c, t, x * ny : (x + 1) * ny, :] = slab[x](c, slice(t * ez, (t + 1) * ez))
            for j in range(order):
                parts = [
                    permute(rows[c, t, pl.ds(j, brick.rows, stride=order), :], gather_index)
                    for t in range(order)
                ]
                for k in range(order):
                    total = parts[0]
                    for t in range(1, order):
                        total = jnp.where(tile_of[k] == t, parts[t], total)
                    put(c, j, k, roll(total, -spread * k, 1))

    pl.semaphore_wait(barrier, sum(exists(shift).astype(jnp.int32) for shift in partners))
    start(round1x)

    def split(i, carry):
        for x in range(ex):
            n = x * order + i
            pltpu.make_async_copy(v_ref.at[:, n], raw.at[:, n], load_sem.at[n]).wait()

        def reader(x):
            return lambda c, lanes: raw[c, x * order + i, :, lanes]

        def put(c, j, k, value):
            vel[c, i, j, k] = value

        split_layer({x: reader(x) for x in range(ex)}, rows_buf.at[i], put)
        return carry

    lax.fori_loop(0, order, split, 0)

    clear(round1x)
    clear(round1)
    clear(round2)
    clear(round3)
    faces = order * order

    def face_of(ref, a, l):
        index = ((l,), (slice(None), l), (slice(None), slice(None), l))[a]
        return ref[index]

    for a in (2, 1):
        for s in range(2):
            l = order - 1 if s == 0 else 0
            face = jnp.concatenate(
                [face_of(vel.at[c], a, l).reshape(faces, brick.rows, ez) for c in range(3)]
            )
            send1[2 * (a - 1) + s][...] = brick.pack(face, a, s == 0)
        start(round1[2 * (a - 1) : 2 * a])

    def inner_axis(a):
        def run(m, carry):
            normal = [vel[(a,) + at_line(a, l, m)] for l in range(order)]
            for c in range(3):
                if c == a:
                    flux = [x * x for x in normal]
                else:
                    flux = [normal[l] * vel[(c,) + at_line(a, l, m)] for l in range(order)]
                out = lifted_derivative(flux)
                for l in range(order):
                    where = (c,) + at_line(a, l, m)
                    conv[where] = out[l] if a == 0 else conv[where] + out[l]
            return carry

        lax.fori_loop(0, order, run, 0)

    for a in range(3):
        inner_axis(a)

    for copy in small:
        copy.wait()
    solid = jnp.concatenate([mask_buf[x] for x in range(ex)], axis=0).astype(jnp.float32)
    scale = jnp.concatenate([scale_buf[x] for x in range(ex)], axis=0)
    fluid = 1.0 / (1.0 + penalty * solid)

    def face_terms(a, components=(0, 1, 2)):
        for s in range(2):
            up = s == 0
            edge = brick.edge(a, up)
            own, other = (0, order - 1) if up else (order - 1, 0)
            for c in components:
                for m in range(order):
                    line = vel[(c,) + at_line(a, other, m)]
                    for q in range(order):
                        n = (c * order + m) * order + q
                        if a == 0:
                            far = far_x[c, m, q]
                        else:
                            far = brick.entry(recv1[2 * (a - 1) + s], n, a, up)
                        near[s, c, m, q] = jnp.where(edge, far, brick.move(line[q], a, up))

            def add_faces(m, carry):
                normal = vel[(a,) + at_line(a, own, m)]
                normal_out = near[s, a, m]
                speed = jnp.maximum(jnp.abs(normal), jnp.abs(normal_out))
                for c in components:
                    moved = vel[(c,) + at_line(a, own, m)]
                    moved_out = near[s, c, m]
                    jump = speed * (moved_out - moved)
                    flux = normal_out * moved_out
                    where = (c,) + at_line(a, own, m)
                    if up:
                        conv[where] = conv[where] - half_lift * (flux + jump)
                    else:
                        conv[where] = conv[where] + half_lift * (flux - jump)
                return carry

            lax.fori_loop(0, order, add_faces, 0, unroll=True)

    def advance(c, i):
        conv[c, i] = (vel[c, i] - time_step * conv[c, i]) * fluid

    for a in (2, 1):
        arrive(round1[2 * (a - 1) : 2 * a])
        face_terms(a)
    for c in range(3):
        for i in range(1, order - 1):
            advance(c, i)

    def reader_x(side):
        return lambda c, lanes: raw_x[side, c, :, lanes]

    def put_x(c, j, k, value):
        far_x[c, j, k] = value

    for a in range(3):
        arrive(round1x[2 * a : 2 * a + 2])
        split_layer({0: reader_x(0), ex - 1: reader_x(1)}, rows_buf.at[0], put_x, (a,))
        face_terms(0, (a,))
        advance(a, 0)
        advance(a, order - 1)
        for s in range(2):
            l = order - 1 if s == 0 else 0
            face = face_of(conv.at[a], a, l).reshape(faces, brick.rows, ez)
            send2[2 * a + s][...] = brick.pack(face, a, s == 0)
        start(round2[2 * a : 2 * a + 2])

        def diverge(m, carry):
            out = lifted_derivative([conv[(a,) + at_line(a, l, m)] for l in range(order)])
            for l in range(order):
                where = at_line(a, l, m)
                pres[where] = -out[l] if a == 0 else pres[where] - out[l]
            return carry

        lax.fori_loop(0, order, diverge, 0, unroll=True)

    for a in range(3):
        arrive(round2[2 * a : 2 * a + 2])
        for s in range(2):
            up = s == 0
            edge = brick.edge(a, up)
            own, other = (0, order - 1) if up else (order - 1, 0)
            for m in range(order):
                line = conv[(a,) + at_line(a, other, m)]
                values = []
                for q in range(order):
                    far = brick.entry(recv2[2 * a + s], m * order + q, a, up)
                    values.append(jnp.where(edge, far, brick.move(line[q], a, up)))
                side = jnp.stack(values)
                where = at_line(a, own, m)
                if up:
                    pres[where] = pres[where] + half_lift * side
                else:
                    pres[where] = pres[where] - half_lift * side

    hats = hat_weight_table()
    by_x = []
    for i in range(order):
        slab = [pres[i, j] for j in range(order)]
        along_y = [mix(hats[b], slab) for b in range(2)]
        by_x.append([[mix(hats[c], [along_y[b][k] for k in range(order)]) for c in range(2)] for b in range(2)])
    parts = {
        (a, b, c): mix(hats[a], [by_x[i][b][c] for i in range(order)])
        for a in range(2)
        for b in range(2)
        for c in range(2)
    }
    for a in (2, 1, 0):
        edge = brick.edge(a, True)
        merged = {}
        for key in parts:
            if key[a] == 1:
                continue
            upper = key[:a] + (1,) + key[a + 1 :]
            moved = brick.move(parts[upper], a, True)
            if a == 1:
                swap = roll(parts[upper], 1 - ey, 0)
                moved = jnp.where(edge, swap, moved)
            merged[key] = parts[key] + jnp.where(edge, 0.0, moved)
            merged[upper] = jnp.where(edge, moved, 0.0)
        parts = merged
    for n, shift in enumerate(corners):
        send3[n] = parts[shift]
    start(round3)

    basis_values = eigen_value_table()

    def forward(i, carry):
        slab = to_modes([pres[i, j] for j in range(order)])
        for j in range(order):
            out = to_modes([slab[j][k] for k in range(order)])
            for k in range(order):
                pres[i, j, k] = out[k]
        return carry

    lax.fori_loop(0, order, forward, 0)

    for j in range(order):
        modes = to_modes([pres[i, j] for i in range(order)])
        scaled = []
        for i in range(order):
            denominator = jnp.stack(
                [
                    scale * float(basis_values[i] + basis_values[j] + basis_values[k]) + 1.0
                    for k in range(order)
                ]
            )
            scaled.append(modes[i] / denominator)
        out = from_modes(scaled)
        for i in range(order):
            pres[i, j] = out[i]

    def backward(i, carry):
        slab = from_modes([pres[i, j] for j in range(order)])
        for j in range(order):
            out = from_modes([slab[j][k] for k in range(order)])
            rolled = [roll(out[k], spread * k, 1) for k in range(order)]
            for t in range(order):
                total = rolled[0]
                for k in range(1, order):
                    total = jnp.where(tile_of[k] == t, rolled[k], total)
                rows_buf[i, 0, t, pl.ds(j, brick.rows, stride=order), :] = permute(
                    total, scatter_index
                )
        for t in range(order):
            for x in range(ex):
                smooth_ref[x * order + i, :, t * ez : (t + 1) * ez] = rows_buf[
                    i, 0, t, x * ny : (x + 1) * ny, :
                ]
        return carry

    lax.fori_loop(0, order, backward, 0)

    arrive(round3)
    total = parts[(0, 0, 0)]
    for n in range(len(corners)):
        total = total + recv3[n]
    for x in range(ex):
        coarse_ref[x] = total[x * ey : (x + 1) * ey]
    finish(round1x)
    finish(round1)
    finish(round2)
    finish(round3)


def shards(counts, velocity, mask, scale):
    ex, ey, ez = mask.shape
    brick = Brick(ex, ey, ez)
    tile = (brick.rows, ez)
    faces = order * order

    def buffers(n):
        return [
            pltpu.VMEM((brick.packed(a, n),) + tile, jnp.float32)
            for a in range(3)
            for _ in range(2)
        ]

    whole = pl.BlockSpec(memory_space=pltpu.VMEM)
    remote = pl.BlockSpec(memory_space=pltpu.HBM)
    sems = pltpu.SemaphoreType.DMA
    f32 = jnp.float32
    layer = velocity.shape[2:]
    return pl.pallas_call(
        functools.partial(body, brick, counts),
        out_shape=(
            jax.ShapeDtypeStruct(velocity.shape[1:], f32),
            jax.ShapeDtypeStruct(mask.shape, f32),
        ),
        in_specs=[remote] * 3,
        out_specs=(whole, whole),
        scratch_shapes=[
            pltpu.VMEM(velocity.shape, f32),
            pltpu.VMEM(mask.shape, jnp.int32),
            pltpu.VMEM(scale.shape, f32),
            pltpu.VMEM((order, 3, order, brick.rows * order, ez), f32),
            pltpu.VMEM((3, order, order, order) + tile, f32),
            pltpu.VMEM((3, order, order, order) + tile, f32),
            pltpu.VMEM((2, 3, order, order) + tile, f32),
            pltpu.VMEM((3, order, order) + tile, f32),
            pltpu.VMEM((order, order, order) + tile, f32),
            pltpu.VMEM((2, 3) + layer, f32),
        ]
        + buffers(3 * faces)[2:]
        + buffers(3 * faces)[2:]
        + buffers(faces)
        + buffers(faces)
        + [pltpu.VMEM((len(corners),) + tile, f32)] * 2
        + [sems((6,))] * 4
        + [sems((len(corners),))] * 2
        + [sems((ex * order,)), sems((2,)), sems((6,)), sems((6,))],
        compiler_params=pltpu.CompilerParams(
            collective_id=0, has_side_effects=True, vmem_limit_bytes=67043328
        ),
    )(velocity, mask, scale)


def solution(mesh):
    counts = tuple(mesh.shape[name] for name in names)
    return jax.shard_map(
        functools.partial(shards, counts),
        mesh=mesh,
        in_specs=(P(None, "gx", "gy", "gz"), P("gx", "gy", "gz"), P("gx", "gy", "gz")),
        out_specs=(P("gx", "gy", "gz"), P("gx", "gy", "gz")),
        check_vma=False,
    )
```

```python
import functools
import itertools
import math

import jax
import jax.numpy as jnp
import numpy as np
from jax import lax
from jax.experimental import pallas as pl
from jax.experimental.pallas import tpu as pltpu
from jax.sharding import PartitionSpec as P

lift_factor = 10.0
time_step = 0.05
penalty = 4.0
half_lift = lift_factor * 0.5
order = 5
names = ("gx", "gy", "gz")
corners = [s for s in itertools.product((0, 1), repeat=3) if any(s)]


def lobatto_points():
    return np.array([-1.0, -math.sqrt(3.0 / 7.0), 0.0, math.sqrt(3.0 / 7.0), 1.0])


def lobatto_weights():
    return np.array([0.1, 49.0 / 90.0, 32.0 / 45.0, 49.0 / 90.0, 0.1])


def derivative_matrix():
    points = lobatto_points()
    scales = np.array(
        [np.prod([points[i] - points[k] for k in range(5) if k != i]) for i in range(5)]
    )
    result = np.zeros((5, 5))
    for i in range(5):
        for j in range(5):
            if i != j:
                result[i, j] = scales[i] / (scales[j] * (points[i] - points[j]))
        result[i, i] = -np.sum(result[i])
    return result


def eigen_basis_table():
    return np.array(
        [
            [
                math.sqrt((1.0 if k == 0 else 2.0) / 5.0) * math.cos(math.pi * (i + 0.5) * k / 5.0)
                for k in range(5)
            ]
            for i in range(5)
        ]
    )


def eigen_value_table():
    return np.array([4.0 * math.sin(math.pi * k / 10.0) ** 2 for k in range(5)])


def hat_weight_table():
    points = lobatto_points()
    weights = lobatto_weights()
    return np.array([weights * (1.0 - points) / 2.0, weights * (1.0 + points) / 2.0])


def mix(coefs, terms):
    total = None
    for coef, term in zip(coefs, terms):
        if abs(coef) < 1e-12:
            continue
        piece = float(coef) * term
        total = piece if total is None else total + piece
    return total


def lifted_derivative(f):
    d = derivative_matrix()
    d[0, 0] += half_lift
    d[4, 4] -= half_lift
    e1, e2 = f[0] + f[4], f[1] + f[3]
    o1, o2 = f[0] - f[4], f[1] - f[3]
    out = [None] * 5
    for i in range(2):
        even = mix(((d[i, 0] + d[i, 4]) / 2, (d[i, 1] + d[i, 3]) / 2, d[i, 2]), (e1, e2, f[2]))
        odd = mix(((d[i, 0] - d[i, 4]) / 2, (d[i, 1] - d[i, 3]) / 2), (o1, o2))
        out[i] = odd + even
        out[4 - i] = odd - even
    out[2] = mix((d[2, 0], d[2, 1]), (o1, o2))
    return out


def to_modes(f):
    s = eigen_basis_table()
    e1, e2 = f[0] + f[4], f[1] + f[3]
    o1, o2 = f[0] - f[4], f[1] - f[3]
    out = []
    for k in range(5):
        if k == 0:
            out.append(float(s[0, 0]) * (e1 + e2 + f[2]))
        elif k % 2 == 0:
            out.append(mix((s[0, k], s[1, k], s[2, k]), (e1, e2, f[2])))
        else:
            out.append(mix((s[0, k], s[1, k]), (o1, o2)))
    return out


def from_modes(c):
    s = eigen_basis_table()
    out = [None] * 5
    base = float(s[0, 0]) * c[0]
    for i in range(2):
        even = base + mix((s[i, 2], s[i, 4]), (c[2], c[4]))
        odd = mix((s[i, 1], s[i, 3]), (c[1], c[3]))
        out[i] = even + odd
        out[4 - i] = even - odd
    out[2] = base + mix((s[2, 2], s[2, 4]), (c[2], c[4]))
    return out


def at_line(a, l, m):
    return ((l, m), (m, l), (m, slice(None), l))[a]


def roll(x, shift, axis):
    size = x.shape[axis]
    shift = shift % size
    return x if shift == 0 else pltpu.roll(x, shift, axis)


class Brick:
    def __init__(self, ex, ey, ez):
        self.ex, self.ey, self.ez = ex, ey, ez
        self.rows = ex * ey

    def iotas(self):
        row = lax.broadcasted_iota(jnp.int32, (self.rows, self.ez), 0)
        lane = lax.broadcasted_iota(jnp.int32, (self.rows, self.ez), 1)
        return row, lane

    def slots(self, a):
        return (self.ex, self.ey, self.ez)[a]

    def packed(self, a, n):
        return -(-n // self.slots(a))

    def step(self, a):
        return (self.ey, 1, 1)[a]

    def place(self, a):
        row, lane = self.iotas()
        return (row // self.ey, row % self.ey, lane)[a]

    def pack(self, face, a, up):
        n = face.shape[0]
        slots, step = self.slots(a), self.step(a)
        axis = 2 if a == 2 else 1
        place = self.place(a)
        start = slots - 1 if up else 0
        groups = []
        if a == 2:
            total = jnp.zeros((self.rows, self.ez), jnp.float32)
            for s in range(n):
                total = jnp.where(place == s, roll(face[s], s - start, 1), total)
            return total[None]
        for g in range(self.packed(a, n)):
            total = None
            for s in range(min(slots, n - g * slots)):
                piece = roll(face[g * slots + s], (s - start) * step, 0)
                total = piece if total is None else jnp.where(place == s, piece, total)
            groups.append(total)
        return jnp.stack(groups)

    def entry(self, packed_ref, n, a, up):
        slots, step = self.slots(a), self.step(a)
        target = 0 if up else slots - 1
        g, s = divmod(n, slots)
        return roll(packed_ref[g], (target - s) * step, 1 if a == 2 else 0)

    def move(self, x, a, up):
        step = self.step(a) if up else -self.step(a)
        return roll(x, step, 1 if a == 2 else 0)

    def edge(self, a, up):
        return self.place(a) == (0 if up else self.slots(a) - 1)


def body(
    brick,
    counts,
    v_ref,
    mask_ref,
    scale_ref,
    smooth_ref,
    coarse_ref,
    raw,
    mask_buf,
    scale_buf,
    rows_buf,
    vel,
    conv,
    near,
    far_x,
    pres,
    raw_x,
    *rest,
):
    send1, recv1, send2, recv2 = rest[0:4], rest[4:8], rest[8:14], rest[14:20]
    send3, recv3 = rest[20], rest[21]
    ssem1, rsem1, ssem2, rsem2, ssem3, rsem3, load_sem, small_sem, ssemx, rsemx = rest[
        22:32
    ]
    ex, ey, ez = brick.ex, brick.ey, brick.ez
    ny = ey * order
    me = [lax.axis_index(name) for name in names]

    def offset_id(shift):
        return tuple(me[a] + shift[a] for a in range(3))

    def exists(shift):
        ok = None
        for a in range(3):
            if shift[a] > 0:
                one = me[a] < counts[a] - 1
            elif shift[a] < 0:
                one = me[a] > 0
            else:
                continue
            ok = one if ok is None else jnp.logical_and(ok, one)
        return ok

    layers = ex * order
    loads = [
        pltpu.make_async_copy(v_ref.at[:, n], raw.at[:, n], load_sem.at[n]) for n in range(layers)
    ]
    small = [
        pltpu.make_async_copy(mask_ref, mask_buf, small_sem.at[0]),
        pltpu.make_async_copy(scale_ref, scale_buf, small_sem.at[1]),
    ]

    unit = [tuple(int(a == b) for b in range(3)) for a in range(3)]
    partners = unit + [tuple(-x for x in u) for u in unit]
    barrier = pltpu.get_barrier_semaphore()
    for shift in partners:

        @pl.when(exists(shift))
        def _():
            pl.semaphore_signal(
                barrier,
                inc=1,
                device_id=offset_id(shift),
                device_id_type=pl.DeviceIdType.MESH,
            )

    for i in range(order):
        for x in range(ex):
            loads[x * order + i].start()
    for copy in small:
        copy.start()

    def transfer(src, dst, ssem, rsem, to):
        copy = pltpu.make_async_remote_copy(
            src_ref=src,
            dst_ref=dst,
            send_sem=ssem,
            recv_sem=rsem,
            device_id=offset_id(to),
            device_id_type=pl.DeviceIdType.MESH,
        )
        return (copy, exists(to), exists(tuple(-x for x in to)), dst)

    def copies(send, recv, ssem, rsem, axes):
        out = []
        for n, a in enumerate(axes):
            for s in range(2):
                d = 2 * n + s
                to = tuple((1 - 2 * s) * u for u in unit[a])
                out.append(transfer(send[d], recv[d], ssem.at[d], rsem.at[d], to))
        return out

    def start(group):
        for copy, has_to, has_source, _ in group:

            @pl.when(has_to)
            def _():
                copy.start()

    def clear(group):
        for _, _, has_source, dst in group:

            @pl.when(jnp.logical_not(has_source))
            def _():
                dst[...] = jnp.zeros_like(dst)

    def arrive(group):
        for copy, has_to, has_source, _ in group:

            @pl.when(has_source)
            def _():
                copy.wait_recv()

    def finish(group):
        for copy, has_to, has_source, _ in group:

            @pl.when(has_to)
            def _():
                copy.wait_send()

    round1x = []
    for c in range(3):
        for s, n in enumerate((layers - 1, 0)):
            to = tuple((1 - 2 * s) * u for u in unit[0])
            d = 2 * c + s
            round1x.append(
                transfer(v_ref.at[c, n], raw_x.at[s, c], ssemx.at[d], rsemx.at[d], to)
            )
    round1 = copies(send1, recv1, ssem1, rsem1, (1, 2))
    round2 = copies(send2, recv2, ssem2, rsem2, (0, 1, 2))
    round3 = [
        transfer(send3.at[n], recv3.at[n], ssem3.at[n], rsem3.at[n], shift)
        for n, shift in enumerate(corners)
    ]

    row, lane = brick.iotas()
    spread = pow(order, -1, ez)
    gather_index = (lane * order) % ez
    scatter_index = (lane * spread) % ez

    def permute(x, index):
        return jnp.take_along_axis(x, index, axis=1, mode="promise_in_bounds")

    tile_of = [(((lane - spread * k) % ez) * order + k) // ez for k in range(order)]

    def split_layer(slab, rows, put, components=(0, 1, 2)):
        for c in components:
            for t in range(order):
                for x in slab:
                    rows[c, t, x * ny : (x + 1) * ny, :] = slab[x](c, slice(t * ez, (t + 1) * ez))
            for j in range(order):
                parts = [
                    permute(rows[c, t, pl.ds(j, brick.rows, stride=order), :], gather_index)
                    for t in range(order)
                ]
                for k in range(order):
                    total = parts[0]
                    for t in range(1, order):
                        total = jnp.where(tile_of[k] == t, parts[t], total)
                    put(c, j, k, roll(total, -spread * k, 1))

    def split(i, carry):
        for x in range(ex):
            n = x * order + i
            pltpu.make_async_copy(v_ref.at[:, n], raw.at[:, n], load_sem.at[n]).wait()

        def reader(x):
            return lambda c, lanes: raw[c, x * order + i, :, lanes]

        def put(c, j, k, value):
            vel[c, i, j, k] = value

        split_layer({x: reader(x) for x in range(ex)}, rows_buf.at[i], put)
        return carry

    lax.fori_loop(0, 2, split, 0)
    pl.semaphore_wait(barrier, sum(exists(shift).astype(jnp.int32) for shift in partners))
    start(round1x)
    lax.fori_loop(2, order, split, 0)

    clear(round1x)
    clear(round1)
    clear(round2)
    clear(round3)
    faces = order * order

    def face_of(ref, a, l):
        index = ((l,), (slice(None), l), (slice(None), slice(None), l))[a]
        return ref[index]

    for a in (2, 1):
        for s in range(2):
            l = order - 1 if s == 0 else 0
            face = jnp.concatenate(
                [face_of(vel.at[c], a, l).reshape(faces, brick.rows, ez) for c in range(3)]
            )
            send1[2 * (a - 1) + s][...] = brick.pack(face, a, s == 0)
        start(round1[2 * (a - 1) : 2 * a])

    def inner_axis(a):
        def run(m, carry):
            normal = [vel[(a,) + at_line(a, l, m)] for l in range(order)]
            for c in range(3):
                if c == a:
                    flux = [x * x for x in normal]
                else:
                    flux = [normal[l] * vel[(c,) + at_line(a, l, m)] for l in range(order)]
                out = lifted_derivative(flux)
                for l in range(order):
                    where = (c,) + at_line(a, l, m)
                    conv[where] = out[l] if a == 0 else conv[where] + out[l]
            return carry

        lax.fori_loop(0, order, run, 0)

    for a in range(3):
        inner_axis(a)

    for copy in small:
        copy.wait()
    solid = jnp.concatenate([mask_buf[x] for x in range(ex)], axis=0).astype(jnp.float32)
    scale = jnp.concatenate([scale_buf[x] for x in range(ex)], axis=0)
    fluid = 1.0 / (1.0 + penalty * solid)

    def face_terms(a, components=(0, 1, 2)):
        for s in range(2):
            up = s == 0
            edge = brick.edge(a, up)
            own, other = (0, order - 1) if up else (order - 1, 0)
            for c in components:
                for m in range(order):
                    line = vel[(c,) + at_line(a, other, m)]
                    for q in range(order):
                        n = (c * order + m) * order + q
                        if a == 0:
                            far = far_x[c, m, q]
                        else:
                            far = brick.entry(recv1[2 * (a - 1) + s], n, a, up)
                        near[s, c, m, q] = jnp.where(edge, far, brick.move(line[q], a, up))

            def add_faces(m, carry):
                normal = vel[(a,) + at_line(a, own, m)]
                normal_out = near[s, a, m]
                speed = jnp.maximum(jnp.abs(normal), jnp.abs(normal_out))
                for c in components:
                    moved = vel[(c,) + at_line(a, own, m)]
                    moved_out = near[s, c, m]
                    jump = speed * (moved_out - moved)
                    flux = normal_out * moved_out
                    where = (c,) + at_line(a, own, m)
                    if up:
                        conv[where] = conv[where] - half_lift * (flux + jump)
                    else:
                        conv[where] = conv[where] + half_lift * (flux - jump)
                return carry

            lax.fori_loop(0, order, add_faces, 0, unroll=True)

    def advance(c, i):
        conv[c, i] = (vel[c, i] - time_step * conv[c, i]) * fluid

    for a in (2, 1):
        arrive(round1[2 * (a - 1) : 2 * a])
        face_terms(a)
    for c in range(3):
        for i in range(1, order - 1):
            advance(c, i)

    def reader_x(side):
        return lambda c, lanes: raw_x[side, c, :, lanes]

    def put_x(c, j, k, value):
        far_x[c, j, k] = value

    for a in range(3):
        arrive(round1x[2 * a : 2 * a + 2])
        split_layer({0: reader_x(0), ex - 1: reader_x(1)}, rows_buf.at[0], put_x, (a,))
        face_terms(0, (a,))
        advance(a, 0)
        advance(a, order - 1)
        for s in range(2):
            l = order - 1 if s == 0 else 0
            face = face_of(conv.at[a], a, l).reshape(faces, brick.rows, ez)
            send2[2 * a + s][...] = brick.pack(face, a, s == 0)
        start(round2[2 * a : 2 * a + 2])

    for a in range(3):

        def diverge(m, carry):
            out = lifted_derivative([conv[(a,) + at_line(a, l, m)] for l in range(order)])
            for l in range(order):
                where = at_line(a, l, m)
                pres[where] = -out[l] if a == 0 else pres[where] - out[l]
            return carry

        lax.fori_loop(0, order, diverge, 0, unroll=True)

    for a in range(3):
        arrive(round2[2 * a : 2 * a + 2])
        for s in range(2):
            up = s == 0
            edge = brick.edge(a, up)
            own, other = (0, order - 1) if up else (order - 1, 0)
            for m in range(order):
                line = conv[(a,) + at_line(a, other, m)]
                values = []
                for q in range(order):
                    far = brick.entry(recv2[2 * a + s], m * order + q, a, up)
                    values.append(jnp.where(edge, far, brick.move(line[q], a, up)))
                side = jnp.stack(values)
                where = at_line(a, own, m)
                if up:
                    pres[where] = pres[where] + half_lift * side
                else:
                    pres[where] = pres[where] - half_lift * side

    hats = hat_weight_table()
    by_x = []
    for i in range(order):
        slab = [pres[i, j] for j in range(order)]
        along_y = [mix(hats[b], slab) for b in range(2)]
        by_x.append([[mix(hats[c], [along_y[b][k] for k in range(order)]) for c in range(2)] for b in range(2)])
    parts = {
        (a, b, c): mix(hats[a], [by_x[i][b][c] for i in range(order)])
        for a in range(2)
        for b in range(2)
        for c in range(2)
    }
    for a in (2, 1, 0):
        edge = brick.edge(a, True)
        merged = {}
        for key in parts:
            if key[a] == 1:
                continue
            upper = key[:a] + (1,) + key[a + 1 :]
            moved = brick.move(parts[upper], a, True)
            if a == 1:
                swap = roll(parts[upper], 1 - ey, 0)
                moved = jnp.where(edge, swap, moved)
            merged[key] = parts[key] + jnp.where(edge, 0.0, moved)
            merged[upper] = jnp.where(edge, moved, 0.0)
        parts = merged
    for n, shift in enumerate(corners):
        send3[n] = parts[shift]
    start(round3)

    basis_values = eigen_value_table()

    def forward(i, carry):
        slab = to_modes([pres[i, j] for j in range(order)])
        for j in range(order):
            out = to_modes([slab[j][k] for k in range(order)])
            for k in range(order):
                pres[i, j, k] = out[k]
        return carry

    lax.fori_loop(0, order, forward, 0)

    for j in range(order):
        modes = to_modes([pres[i, j] for i in range(order)])
        scaled = []
        for i in range(order):
            denominator = jnp.stack(
                [
                    scale * float(basis_values[i] + basis_values[j] + basis_values[k]) + 1.0
                    for k in range(order)
                ]
            )
            scaled.append(modes[i] / denominator)
        out = from_modes(scaled)
        for i in range(order):
            pres[i, j] = out[i]

    def backward(i, carry):
        slab = from_modes([pres[i, j] for j in range(order)])
        for j in range(order):
            out = from_modes([slab[j][k] for k in range(order)])
            rolled = [roll(out[k], spread * k, 1) for k in range(order)]
            for t in range(order):
                total = rolled[0]
                for k in range(1, order):
                    total = jnp.where(tile_of[k] == t, rolled[k], total)
                rows_buf[i, 0, t, pl.ds(j, brick.rows, stride=order), :] = permute(
                    total, scatter_index
                )
        for t in range(order):
            for x in range(ex):
                smooth_ref[x * order + i, :, t * ez : (t + 1) * ez] = rows_buf[
                    i, 0, t, x * ny : (x + 1) * ny, :
                ]
        return carry

    lax.fori_loop(0, order, backward, 0)

    arrive(round3)
    total = parts[(0, 0, 0)]
    for n in range(len(corners)):
        total = total + recv3[n]
    for x in range(ex):
        coarse_ref[x] = total[x * ey : (x + 1) * ey]
    finish(round1x)
    finish(round1)
    finish(round2)
    finish(round3)


def shards(counts, velocity, mask, scale):
    ex, ey, ez = mask.shape
    brick = Brick(ex, ey, ez)
    tile = (brick.rows, ez)
    faces = order * order

    def buffers(n):
        return [
            pltpu.VMEM((brick.packed(a, n),) + tile, jnp.float32)
            for a in range(3)
            for _ in range(2)
        ]

    whole = pl.BlockSpec(memory_space=pltpu.VMEM)
    remote = pl.BlockSpec(memory_space=pltpu.HBM)
    sems = pltpu.SemaphoreType.DMA
    f32 = jnp.float32
    layer = velocity.shape[2:]
    kept = 4 * velocity.size * 1 // 1
    return pl.pallas_call(
        functools.partial(body, brick, counts),
        out_shape=(
            jax.ShapeDtypeStruct(velocity.shape[1:], f32),
            jax.ShapeDtypeStruct(mask.shape, f32),
        ),
        in_specs=[remote] * 3,
        out_specs=(whole, whole),
        scratch_shapes=[
            pltpu.VMEM(velocity.shape, f32),
            pltpu.VMEM(mask.shape, jnp.int32),
            pltpu.VMEM(scale.shape, f32),
            pltpu.VMEM((order, 3, order, brick.rows * order, ez), f32),
            pltpu.VMEM((3, order, order, order) + tile, f32),
            pltpu.VMEM((3, order, order, order) + tile, f32),
            pltpu.VMEM((2, 3, order, order) + tile, f32),
            pltpu.VMEM((3, order, order) + tile, f32),
            pltpu.VMEM((order, order, order) + tile, f32),
            pltpu.VMEM((2, 3) + layer, f32),
        ]
        + buffers(3 * faces)[2:]
        + buffers(3 * faces)[2:]
        + buffers(faces)
        + buffers(faces)
        + [pltpu.VMEM((len(corners),) + tile, f32)] * 2
        + [sems((6,))] * 4
        + [sems((len(corners),))] * 2
        + [sems((ex * order,)), sems((2,)), sems((6,)), sems((6,))],
        compiler_params=pltpu.CompilerParams(
            collective_id=0, has_side_effects=True, vmem_limit_bytes=67043328 - kept
        ),
    )(velocity, mask, scale)


def solution(mesh):
    counts = tuple(mesh.shape[name] for name in names)
    return jax.shard_map(
        functools.partial(shards, counts),
        mesh=mesh,
        in_specs=(P(None, "gx", "gy", "gz"), P("gx", "gy", "gz"), P("gx", "gy", "gz")),
        out_specs=(P("gx", "gy", "gz"), P("gx", "gy", "gz")),
        check_vma=False,
    )
```
